32 devices in a mesh: groups: 2 (over y), date: 4 (over x, core), col: 4 (over z).
Axes of the slice: x: 2, y: 2, z: 4, core: 2. Of those that a mesh axis runs over, the one named last changes fastest.
Arguments:
- scenes: bfloat16 [16, 2, 128, 1024], P('date', None, 'groups', 'col'), parts along dimension 2, may hold values from -6 to 6
- pair_dates: int32 [96, 2], P('date'), may hold values from 0 to 15, as said below
- pair_count: int32 [4], P('date'), may hold values from 12 to 24, as said below
- inverse: float32 [15, 96], replicated, may hold values from -0.625 to 0.625
Outputs:
- series: float32 [15, 2, 64, 128], P(None, None, ('groups', 'date'), 'col'), parts along dimension 2
The draws below stay inside these ranges and needn't reach their ends.
There are 2 independent parts, one for each index of `groups`. The reference program is written for one: setup_inputs(seed, part) draws one part's arguments, and reference() takes and returns one part's arrays. A program takes and returns all parts, laid end to end along the dimension named above; an argument that names none is the same for every part. Nothing has to cross between parts.
Inputs may be any that keep to these rules, and one draw needn't show every extreme that they name: `pair_dates`: each row names a reference acquisition and a later secondary one. Slots i * 24 to (i + 1) * 24 - 1 belong to owner i (index i of date); every slot of owner i names acquisitions held by indices i - 2 to i + 2 of date (as far as these exist), and one live pair of every owner names the lowest and the highest acquisition of that range. `pair_count`: entry i is the number of live slots of owner i; they come first in its block and the other slots are ignored. Some owner has all its slots live.
All inputs are finite; a program needn't handle non-finite values.
Results may differ from the reference program's by a relative error of at most 0.0003.
Values may be sent and summed in bfloat16 or wider, within the bound.
A program may use at most 64 MiB of HBM per device.

```python
import jax
import jax.numpy as jnp
from jax import lax

DATE_DEV = 4
PAIR_DEV = 24
HOPS = 2
ROWS = 64
DATES = 16
PAIRS = 96
NPAR = 15
COLS = 1024
MLR = 32
MLC = 128


def draw_pair_dates(key, part):
    indices = jnp.arange(PAIRS, dtype=jnp.int32)
    owners = indices // PAIR_DEV
    within = indices % PAIR_DEV
    lowest = jnp.maximum(0, (owners - HOPS) * DATE_DEV)
    highest = jnp.minimum(DATES, (owners + HOPS + 1) * DATE_DEV)
    key_first, key_step = jax.random.split(jax.random.fold_in(key, 11))
    leading = jax.random.randint(key_first, (PAIRS,), lowest, highest - 1)
    stepping = jax.random.randint(key_step, (PAIRS,), 1, 7)
    trailing = jnp.minimum(leading + stepping, highest - 1)
    leading = jnp.where(within == 0, lowest, leading)
    trailing = jnp.where(within == 0, jnp.minimum(lowest + stepping, highest - 1), trailing)
    leading = jnp.where(within == 1, jnp.maximum(lowest, highest - 1 - stepping), leading)
    trailing = jnp.where(within == 1, highest - 1, trailing)
    leading = jnp.where(within == 2, lowest, leading)
    trailing = jnp.where(within == 2, highest - 1, trailing)
    return jnp.stack([leading, trailing], axis=1).astype(jnp.int32)


def draw_pair_count(key, part):
    owner_total = PAIRS // PAIR_DEV
    key_counts, key_full = jax.random.split(jax.random.fold_in(key, 23))
    counts = jax.random.randint(key_counts, (owner_total,), PAIR_DEV // 2, PAIR_DEV + 1)
    busiest = jax.random.randint(key_full, (), 0, owner_total)
    return jnp.where(jnp.arange(owner_total) == busiest, PAIR_DEV, counts).astype(jnp.int32)


def shard_levels(stream_key, dims, cuts, smallest, largest):
    def one(dim, blocks):
        heights = jax.random.uniform(jax.random.fold_in(jax.random.fold_in(stream_key, 6), dim), (blocks,), jnp.float32, smallest / len(cuts), largest / len(cuts))
        return jnp.repeat(jnp.exp(heights), dims[dim] // blocks).reshape((-1,) + (1,) * (len(dims) - dim - 1))

    factor_of = one(*cuts[0])
    for cut in cuts[1:]:
        factor_of = factor_of * one(*cut)
    return factor_of


def noise(own_key, dims, spread, reach, pieces=(), kind=jnp.bfloat16):
    array = spread * jax.random.normal(own_key, dims, jnp.float32)
    if pieces:
        array = array * shard_levels(own_key, dims, pieces, -0.22, 0.18)
    return jnp.clip(array, -reach, reach).astype(kind)


def setup_inputs(seed: int = 0, part: int = 0) -> dict:
    seeds = jax.random.split(jax.random.key(seed), 5)
    part_keys = jax.random.split(jax.random.fold_in(seeds[4], part), 5)
    return {
        "scenes": noise(part_keys[0], (DATES, 2, ROWS, COLS), 1.0, 6.0, ((0, 4), (3, 4))),
        "pair_dates": draw_pair_dates(jax.random.fold_in(seeds[4], 71), part),
        "pair_count": draw_pair_count(jax.random.fold_in(seeds[4], 71), part),
        "inverse": noise(seeds[3], (NPAR, PAIRS), PAIRS ** -0.5, 0.625, (), jnp.float32),
    }


def look_weights():
    offsets = jnp.arange(16).astype(jnp.float32)
    return (8.0 - jnp.abs(offsets - 7.5)) / 64.0


def reference(scenes, pair_dates, pair_count, inverse):
    indices = jnp.arange(PAIRS).astype(jnp.int32)
    owners = indices // PAIR_DEV
    within = indices % PAIR_DEV
    living = (within < pair_count[owners]).astype(jnp.float32)
    weights = look_weights()

    def one_pair(member):
        pair_row, alive = member
        primary = scenes[pair_row[0]].astype(jnp.float32)
        secondary = scenes[pair_row[1]].astype(jnp.float32)
        real_part = primary[0] * secondary[0] + primary[1] * secondary[1]
        imaginary = primary[1] * secondary[0] - primary[0] * secondary[1]
        products = jnp.stack([real_part, imaginary]) * alive
        halved = 0.5 * (products[:, 0::2, :] + products[:, 1::2, :])
        padded = jnp.pad(halved, ((0, 0), (0, 0), (4, 4)))
        looked = jnp.zeros((2, MLR, MLC), jnp.float32)
        for offset in range(16):
            looked = looked + weights[offset] * padded[:, :, offset: offset + COLS: 8]
        return looked

    multilooked = lax.map(one_pair, (pair_dates, living))
    flattened = multilooked.reshape(PAIRS, 2 * MLR * MLC)
    series = jnp.dot(inverse, flattened, precision=lax.Precision.HIGHEST, preferred_element_type=jnp.float32)
    return series.reshape(NPAR, 2, MLR, MLC)
```

```python
import functools

import jax
import jax.numpy as jnp
from jax import lax
from jax.experimental import pallas as pl
from jax.experimental.pallas import tpu as pltpu
from jax.sharding import PartitionSpec as P

MESH = pl.DeviceIdType.MESH
F32 = jnp.float32
BF16 = jnp.bfloat16
EDGE = 4
LANES = 128
SUBLANES = 8


def flipped(place, slot):
    low, high = place % 2, place // 2
    a, b = slot % 2, slot // 2
    return low + a - 2 * low * a + 2 * (high + b - 2 * high * b)


def split(value):
    high = value.astype(BF16)
    return high, (value - high.astype(F32)).astype(BF16)


def iota(shape, dim):
    return lax.broadcasted_iota(jnp.int32, shape, dim)


def turns(group):
    half = group // 2
    inside = [(g, g, n) for g in range(2) for n in range(1, half + 1)]
    return inside[:half] + [(0, 1, n) for n in range(group)] + inside[half:]


def stack_kernel(
    cfg,
    scenes, dates, count, inverse, out,
    local, near, far, dates_in, counts_in, inverse_in, edge_out, edge_in, turned,
    raw_a, raw_b, raw_e, pairs, pairs_e, weights, coef, along, along_e,
    load_sem, own_sem, far_send, far_recv, near_send, near_recv,
    dates_send, dates_recv, count_send, count_recv, edge_send, edge_recv, met_sem, go_sem,
):
    D, C, A, R, X, S, NP = (cfg[k] for k in ("D", "C", "A", "R", "X", "S", "NP"))
    T = X // LANES
    H = R // SUBLANES
    half = R // 2
    part = SUBLANES // 2
    looks = X // 8
    group = D // 2 * A
    order = turns(group)
    height = len(order) * group
    QP = 2 * SUBLANES
    pitch_a, pitch_b, pitch_r = cfg["pitch_a"], cfg["pitch_b"], cfg["pitch_r"]
    date = lax.axis_index("date")
    col = lax.axis_index("col")
    has_left = col > 0
    has_right = col < C - 1
    leads = date == 0
    sides = has_left.astype(jnp.int32) + has_right.astype(jnp.int32)

    def rows_of(place):
        return pl.ds(pl.multiple_of(place * R, R), R)

    barrier = pltpu.get_barrier_semaphore()
    for r in range(D - 1, 0, -1):
        pl.semaphore_signal(barrier, inc=1, device_id={"date": flipped(date, r)}, device_id_type=MESH)

    load = pltpu.make_async_copy(scenes, local, load_sem)
    load.start()
    own = [
        pltpu.make_async_copy(dates, dates_in.at[date], own_sem.at[0]),
        pltpu.make_async_copy(count, counts_in.at[date], own_sem.at[1]),
        pltpu.make_async_copy(inverse, inverse_in, own_sem.at[2]),
    ]
    for copy in own:
        copy.start()

    @pl.when(leads & has_left)
    def _():
        pl.semaphore_signal(barrier, inc=1, device_id={"col": col - 1}, device_id_type=MESH)

    @pl.when(leads & has_right)
    def _():
        pl.semaphore_signal(barrier, inc=1, device_id={"col": col + 1}, device_id_type=MESH)

    pl.semaphore_wait(barrier, D - 1 + leads.astype(jnp.int32) * sides)

    def remote(src, dst, ssem, rsem, device):
        return pltpu.make_async_remote_copy(src_ref=src, dst_ref=dst, send_sem=ssem, recv_sem=rsem, device_id=device, device_id_type=MESH)

    def chunk(n):
        return n // H, n % H

    def send_far(n):
        t, h = chunk(n)
        for r in (2, 3):
            there = flipped(date, r)
            rows = pl.ds(pl.multiple_of(there * R + h * SUBLANES, SUBLANES), SUBLANES)
            remote(scenes.at[:, :, rows, t * LANES:(t + 1) * LANES], far.at[n, r - 2], far_send, far_recv.at[n], {"date": there}).start()

    send_far(0)
    partner = flipped(date, 1)
    to_near = remote(scenes.at[:, :, rows_of(partner), :], near, near_send, near_recv, {"date": partner})
    to_near.start()
    for r in range(D - 1, 0, -1):
        remote(dates, dates_in.at[date], dates_send, dates_recv, {"date": flipped(date, r)}).start()
        remote(count, counts_in.at[date], count_send, count_recv, {"date": flipped(date, r)}).start()
    for n in range(1, T * H):
        send_far(n)

    @pl.when(leads & has_left)
    def _():
        pl.semaphore_signal(met_sem, inc=1, device_id={"col": col - 1}, device_id_type=MESH)

    @pl.when(leads & has_right)
    def _():
        pl.semaphore_signal(met_sem, inc=1, device_id={"col": col + 1}, device_id_type=MESH)

    @pl.when(jnp.logical_not(has_left))
    def _():
        edge_in[0] = jnp.zeros(edge_in.shape[1:], BF16)

    @pl.when(jnp.logical_not(has_right))
    def _():
        edge_in[1] = jnp.zeros(edge_in.shape[1:], BF16)

    load.wait()
    lane = iota((D * R, LANES), 1)
    packed = jnp.zeros((D * R, LANES), F32)
    for i in range(2 * A):
        first = local[i // 2, i % 2, :, 0:LANES].astype(F32)
        last = local[i // 2, i % 2, :, X - LANES:X].astype(F32)
        shift = 2 * EDGE * i + EDGE
        packed = jnp.where(lane // EDGE == 2 * i, pltpu.roll(last, shift, 1), packed)
        packed = jnp.where(lane // EDGE == 2 * i + 1, pltpu.roll(first, shift, 1), packed)
    packed = jnp.concatenate([packed, jnp.zeros((LANES - D * R, LANES), F32)], axis=0)
    turned[...] = jnp.transpose(packed)
    spot = iota((2 * A, LANES), 1) // R
    columns = [turned[pl.ds(n, 2 * A, stride=2 * EDGE), :] for n in range(2 * EDGE)]
    for side in range(2):
        for d in range(D):
            total = jnp.zeros((2 * A, LANES), F32)
            for n in range(side * EDGE, (side + 1) * EDGE):
                shift = (n * R - d * R) % LANES
                total = jnp.where(spot == n, pltpu.roll(columns[n], shift, 1) if shift else columns[n], total)
            edge_out[side, d] = total.astype(BF16)

    @pl.when(leads)
    def _():
        pl.semaphore_wait(met_sem, sides)
        for r in range(1, D):
            pl.semaphore_signal(go_sem, inc=1, device_id={"date": flipped(date, r)}, device_id_type=MESH)

    @pl.when(jnp.logical_not(leads))
    def _():
        pl.semaphore_wait(go_sem, 1)

    def to_side(side, r):
        there = flipped(date, r)
        return remote(edge_out.at[side, there], edge_in.at[side, r], edge_send.at[side], edge_recv.at[side], {"date": there, "col": col + 1 - 2 * side})

    @pl.when(has_right)
    def _():
        for r in range(D - 1, -1, -1):
            to_side(0, r).start()

    @pl.when(has_left)
    def _():
        for r in range(D - 1, -1, -1):
            to_side(1, r).start()

    row = iota(((T + 1) * LANES, LANES), 0)
    at = row - T * LANES
    place = at // R
    column = jnp.where(at < 0, row, jnp.where(place < EDGE, place - EDGE, place - EDGE + X))
    target = iota(((T + 1) * LANES, LANES), 1)
    offset = column - 8 * target + 4
    inside = (target < looks) & (offset >= 0) & (offset < 16)
    weights[...] = jnp.where(inside, (8.0 - jnp.abs(offset.astype(F32) - 7.5)) / 128.0, 0.0).astype(BF16)

    def unpack(raw, pitch, again, c, t, h, index, block):
        start = ((c * T + t) * R + h * SUBLANES) * pitch + index
        raw[pl.ds(start, SUBLANES, stride=pitch), :] = block
        if index < again:
            raw[pl.ds(start + group, SUBLANES, stride=pitch), :] = block

    def unpack_near(of, slot):
        for c in range(2):
            for t in range(T):
                for i in range(A):
                    both = of(i, c, t).astype(F32)
                    for h in range(H):
                        unpack(raw_a, pitch_a, group // 2, c, t, h, slot * A + i, both[h * SUBLANES:(h + 1) * SUBLANES])

    def got(raw, pitch, c, t, r, parity, turn):
        start = ((c * T + t) * R + 2 * r + parity) * pitch + turn
        return raw[pl.ds(start, group), :]

    def four(raw, pitch, t, r, turn):
        return [got(raw, pitch, c, t, r, parity, turn) for parity in range(2) for c in range(2)]

    def product(p, s):
        real = imaginary = None
        for n in range(0, len(p), 2):
            one = p[n] * s[n] + p[n + 1] * s[n + 1]
            two = p[n + 1] * s[n] - p[n] * s[n + 1]
            real = one if real is None else real + one
            imaginary = two if imaginary is None else imaginary + two
        return real, imaginary

    def emit(into, c, at, lanes, values):
        high, low = split(jnp.concatenate(values, axis=0))
        into[c, at:at + 2 * group, lanes] = high
        into[c, height + at:height + at + 2 * group, lanes] = low

    def run(into, lanes, load_of, steps):
        firsts = {}
        for n in steps:
            both = []
            for g, k, turn in order[2 * n:2 * n + 2]:
                if g not in firsts:
                    firsts[g] = load_of(g, 0)
                both.append(product(firsts[g], load_of(k, turn)))
            for c in range(2):
                emit(into, c, 2 * n * group, lanes, [v[c] for v in both])

    def part_of(n, steps):
        t, h = chunk(n)
        for i in range(part):
            r = h * part + i

            def load_of(g, turn):
                return four(raw_b, pitch_b, t, r, turn) if g else four(raw_a, pitch_a, t, r, turn)

            run(pairs.at[n], slice(i * LANES, (i + 1) * LANES), load_of, steps)

    def contract(c, rhs):
        value = jnp.dot(coef[c], rhs, preferred_element_type=F32)
        return value[0:QP] + value[QP:2 * QP]

    early = group // 4
    steps = len(order) // 2

    unpack_near(lambda i, c, t: local[i, c, rows_of(date), t * LANES:(t + 1) * LANES], 0)
    to_near.wait_recv()
    unpack_near(lambda i, c, t: near[i, c, :, t * LANES:(t + 1) * LANES], 1)
    for n in range(T * H):
        part_of(n, range(early))

    for copy in own:
        copy.wait()
    others = pl.ds(0, D - 1)
    pltpu.make_async_copy(dates_in.at[others], dates_in.at[others], dates_recv).wait()
    pltpu.make_async_copy(counts_in.at[others], counts_in.at[others], count_recv).wait()
    coefficients(cfg, date, order, dates_in, counts_in, inverse_in, coef)

    for n in range(T * H):
        t, h = chunk(n)
        pltpu.make_async_copy(far.at[n], far.at[n], far_recv.at[n]).wait()
        for slot in range(2):
            for i in range(A):
                for c in range(2):
                    unpack(raw_b, pitch_b, group - 1, c, t, h, slot * A + i, far[n, slot, i, c].astype(F32))
        part_of(n, range(early, steps))
        for c in range(2):
            value = contract(c, pairs[n, c])
            for i in range(part):
                start = (h * part + i) * pitch_r + c * QP
                along[t, start:start + QP] = value[:, i * LANES:(i + 1) * LANES]

    @pl.when(has_left)
    def _():
        pltpu.make_async_copy(edge_in.at[0], edge_in.at[0], edge_recv.at[0]).wait()

    @pl.when(has_right)
    def _():
        pltpu.make_async_copy(edge_in.at[1], edge_in.at[1], edge_recv.at[1]).wait()

    for slot in range(D):
        value = edge_in[0, slot].astype(F32) + edge_in[1, slot].astype(F32)
        start = slot // 2 * 4 * group + slot % 2 * 2 * A
        raw_e[start:start + 2 * A] = value
        raw_e[start + 2 * group:start + 2 * group + 2 * A] = value

    def edges_of(g, turn):
        return [raw_e[pl.ds(g * 4 * group + c + 2 * turn, group, stride=2), :] for c in range(2)]

    run(pairs_e, slice(0, LANES), edges_of, range(steps))
    for c in range(2):
        along_e[c * QP:(c + 1) * QP] = contract(c, pairs_e[c])

    mine = (iota((half, LANES), 1) % R) // 2 == iota((half, LANES), 0)
    blocks = []
    for q in range(NP):
        for c in range(2):
            main = [along[t, pl.ds(c * QP + q, half, stride=pitch_r), :] for t in range(T)]
            edge = jnp.where(mine, along_e[pl.ds(c * QP + q, half, stride=0), :], 0.0)
            blocks.append(jnp.concatenate(main + [edge], axis=1))
    high, low = split(jnp.concatenate(blocks, axis=0))
    series = jnp.dot(high, weights[...], preferred_element_type=F32)
    series = series + jnp.dot(low, weights[...], preferred_element_type=F32)
    out[...] = series[:, 0:looks].reshape(NP, 2, half, looks)

    pltpu.make_async_copy(far, far, far_send).wait()
    to_near.wait_send()
    pltpu.make_async_copy(dates_in.at[others], dates_in.at[others], dates_send).wait()
    pltpu.make_async_copy(counts_in.at[others], counts_in.at[others], count_send).wait()

    @pl.when(has_right)
    def _():
        pltpu.make_async_copy(edge_out.at[0], edge_out.at[0], edge_send.at[0]).wait()

    @pl.when(has_left)
    def _():
        pltpu.make_async_copy(edge_out.at[1], edge_out.at[1], edge_send.at[1]).wait()


def coefficients(cfg, date, order, dates_in, counts_in, inverse, coef):
    D, A, S, NP = (cfg[k] for k in ("D", "A", "S", "NP"))
    total = D * A
    group = D // 2 * A
    height = len(order) * group
    codes = []
    for d in range(D):
        row = dates_in[d, 0:1, :] * total + dates_in[d, 1:2, :]
        live = iota((1, S), 1) < counts_in[d]
        codes.append(jnp.where(live, row, -1).astype(F32))
    codes.append(jnp.full((SUBLANES - D, S), -1.0, F32))
    table = jnp.concatenate(codes, axis=0)
    table = jnp.concatenate([table, jnp.full((SUBLANES, LANES - S), -1.0, F32)], axis=1)
    spun = jnp.transpose(table)
    code = jnp.concatenate([spun[0:S, d:d + 1] for d in range(D)], axis=0).astype(jnp.int32)

    place = iota((1, height), 1)
    index = place % group
    first, second, valid = index, index, index >= 0
    for n, (g, k, turn) in enumerate(order):
        here = place // group == n
        first = jnp.where(here, g * group + index, first)
        second = jnp.where(here, k * group + (index + turn) % group, second)
        if g == k and 2 * turn == group:
            valid = valid & jnp.logical_not(here & (index >= turn))
    first = flipped(date, first // A) * A + first % A
    second = flipped(date, second // A) * A + second % A
    ahead = first < second
    want = jnp.where(ahead, first * total + second, second * total + first)
    want = jnp.where(valid, want, -2)
    hit = jnp.where(code == want, 1.0, 0.0).astype(BF16)
    high, low = split(jnp.concatenate([inverse[...], jnp.zeros((2 * SUBLANES - NP, D * S), F32)], axis=0))
    value = jnp.dot(high, hit, preferred_element_type=F32) + jnp.dot(low, hit, preferred_element_type=F32)
    for c in range(2):
        high, low = split(value if c == 0 else jnp.where(ahead, value, -value))
        top = jnp.concatenate([high, high], axis=1)
        bottom = jnp.concatenate([low, jnp.zeros_like(low)], axis=1)
        coef[c] = jnp.concatenate([top, bottom], axis=0)


def padded(cells, sides, width):
    for axis, dim in sides:
        count = lax.axis_size(axis)
        ends = count - 1
        head = lax.slice_in_dim(cells, 0, width, axis=dim)
        tail = lax.slice_in_dim(cells, cells.shape[dim] - width, cells.shape[dim], axis=dim)
        cells = jnp.concatenate(
            [
                lax.ppermute(tail, axis, [(i, (i + 1) % count) for i in range(ends)]),
                cells,
                lax.ppermute(head, axis, [((i + 1) % count, i) for i in range(ends)]),
            ],
            axis=dim,
        )
    return cells


def look_matrix(padded_width, looks_here):
    column = jnp.arange(padded_width, dtype=jnp.int32)[:, None]
    target = jnp.arange(looks_here, dtype=jnp.int32)[None, :]
    offset = (column - 8 * target).astype(jnp.float32)
    inside = (offset >= 0.0) & (offset < 16.0)
    return jnp.where(inside, (8.0 - jnp.abs(offset - 7.5)) / 64.0, 0.0)


def plain_device(scenes, pair_dates, pair_count, inverse):
    slot_count = pair_dates.shape[0]
    looks_here = scenes.shape[3] // 8
    base = lax.all_to_all(scenes, "date", split_axis=2, concat_axis=0, tiled=True)
    used_dates, used_counts = (
        lax.all_gather(pair_dates, "date", axis=0, tiled=True),
        lax.all_gather(pair_count, "date", axis=0, tiled=True),
    )
    slot_index = jnp.arange(used_dates.shape[0], dtype=jnp.int32)
    living = (slot_index % slot_count < jnp.take(used_counts, slot_index // slot_count)).astype(
        jnp.float32
    )
    primary = jnp.take(base, used_dates[:, 0], axis=0)
    secondary = jnp.take(base, used_dates[:, 1], axis=0)
    p_real = primary[:, 0].astype(jnp.float32)
    p_imag = primary[:, 1].astype(jnp.float32)
    s_real = secondary[:, 0].astype(jnp.float32)
    s_imag = secondary[:, 1].astype(jnp.float32)
    real_part = p_real * s_real + p_imag * s_imag
    imaginary = p_imag * s_real - p_real * s_imag
    products = jnp.stack([real_part, imaginary], axis=1) * living[:, None, None, None]
    products = padded(products, (("col", 3),), 4)
    pair_total = products.shape[0]
    padded_width = products.shape[3]
    half_rows = products.shape[2] // 2
    halved = products.reshape(pair_total, 2, half_rows, 2, padded_width).sum(axis=3) * 0.5
    looked = jnp.dot(
        halved.reshape(-1, padded_width),
        look_matrix(padded_width, looks_here),
        precision=lax.Precision.HIGHEST,
        preferred_element_type=jnp.float32,
    )
    looked = looked.reshape(pair_total, 2, half_rows, looks_here)
    return jnp.einsum("qk,kcrm->qcrm", inverse, looked, precision=lax.Precision.HIGHEST)


def per_device(scenes, pair_dates, pair_count, inverse):
    D, C = lax.axis_size("date"), lax.axis_size("col")
    A, _, rows, X = scenes.shape
    S, NP = pair_dates.shape[0], inverse.shape[0]
    R = rows // D
    half = R // 2
    fits = D == 4 and 2 * A == SUBLANES and R == 2 * SUBLANES and X % LANES == 0 and X // 8 <= LANES and X <= 4 * LANES
    fits = fits and S % 8 == 0 and S <= LANES and NP <= 2 * SUBLANES and rows <= LANES
    if not fits:
        return plain_device(scenes, pair_dates, pair_count, inverse)
    T, H = X // LANES, R // SUBLANES
    group = D // 2 * A
    height = len(turns(group)) * group
    cfg = dict(D=D, C=C, A=A, R=R, X=X, S=S, NP=NP, pitch_a=group + group // 2 + 1, pitch_b=2 * group - 1, pitch_r=4 * SUBLANES + 1)
    dma, regular = pltpu.SemaphoreType.DMA, pltpu.SemaphoreType.REGULAR
    return pl.pallas_call(
        functools.partial(stack_kernel, cfg),
        out_shape=pltpu.VMEM((NP, 2, half, X // 8), F32),
        in_specs=[pl.BlockSpec(memory_space=pltpu.HBM)] * 4,
        out_specs=pl.BlockSpec(memory_space=pltpu.VMEM),
        scratch_shapes=[
            pltpu.VMEM(scenes.shape, BF16),
            pltpu.VMEM((A, 2, R, X), BF16),
            pltpu.VMEM((T * H, 2, A, 2, SUBLANES, LANES), BF16),
            pltpu.VMEM((D, 2, S), jnp.int32),
            pltpu.VMEM((D, 1, 1), jnp.int32),
            pltpu.VMEM(inverse.shape, F32),
            pltpu.VMEM((2, D, 2 * A, LANES), BF16),
            pltpu.VMEM((2, D, 2 * A, LANES), BF16),
            pltpu.VMEM((LANES, LANES), F32),
            pltpu.VMEM((2 * T * R * cfg["pitch_a"], LANES), F32),
            pltpu.VMEM((2 * T * R * cfg["pitch_b"], LANES), F32),
            pltpu.VMEM((8 * group, LANES), F32),
            pltpu.VMEM((T * H, 2, 2 * height, SUBLANES // 2 * LANES), BF16),
            pltpu.VMEM((2, 2 * height, LANES), BF16),
            pltpu.VMEM(((T + 1) * LANES, LANES), BF16),
            pltpu.VMEM((2, 4 * SUBLANES, 2 * height), BF16),
            pltpu.VMEM((T, half * cfg["pitch_r"], LANES), F32),
            pltpu.VMEM((4 * SUBLANES, LANES), F32),
            dma, dma((3,)), dma, dma((T * H,)), dma, dma,
            dma, dma, dma, dma, dma((2,)), dma((2,)), regular, regular,
        ],
        compiler_params=pltpu.CompilerParams(collective_id=0, has_side_effects=True),
    )(scenes, pair_dates.T, pair_count.reshape(1, 1), inverse)


def solution(mesh):
    placed = (P("date", None, "groups", "col"), P("date", None), P("date"), P())
    return jax.shard_map(
        per_device,
        mesh=mesh,
        in_specs=placed,
        out_specs=P(None, None, ("groups", "date"), "col"),
        check_vma=False,
    )
```

```python
import functools

import jax
import jax.numpy as jnp
from jax import lax
from jax.experimental import pallas as pl
from jax.experimental.pallas import tpu as pltpu
from jax.sharding import PartitionSpec as P

MESH = pl.DeviceIdType.MESH
F32 = jnp.float32
BF16 = jnp.bfloat16
EDGE = 4
LANES = 128
SUBLANES = 8


def flipped(place, slot):
    low, high = place % 2, place // 2
    a, b = slot % 2, slot // 2
    return low + a - 2 * low * a + 2 * (high + b - 2 * high * b)


def split(value):
    high = value.astype(BF16)
    return high, (value - high.astype(F32)).astype(BF16)


def iota(shape, dim):
    return lax.broadcasted_iota(jnp.int32, shape, dim)


def turns(group):
    half = group // 2
    inside = [(g, g, n) for g in range(2) for n in range(1, half + 1)]
    return inside[:half] + [(0, 1, n) for n in range(group)] + inside[half:]


def stack_kernel(
    cfg,
    scenes, dates, count, inverse, out,
    local, near, far, dates_in, counts_in, inverse_in, edge_out, edge_in, turned,
    raw_a, raw_b, raw_e, pairs, pairs_e, weights, coef, along, along_e,
    load_sem, own_sem, far_send, far_recv, near_send, near_recv,
    dates_send, dates_recv, count_send, count_recv, edge_send, edge_recv, met_sem,
):
    D, C, A, R, X, S, NP = (cfg[k] for k in ("D", "C", "A", "R", "X", "S", "NP"))
    T = X // LANES
    H = R // SUBLANES
    half = R // 2
    part = SUBLANES // 2
    W = cfg["W"]
    K = T // W * H
    looks = X // 8
    group = D // 2 * A
    order = turns(group)
    height = len(order) * group
    QP = 2 * SUBLANES
    pitch_a, pitch_b, pitch_r = cfg["pitch_a"], cfg["pitch_b"], cfg["pitch_r"]
    date = lax.axis_index("date")
    col = lax.axis_index("col")
    has_left = col > 0
    has_right = col < C - 1
    odd = col % 2 == 1
    sides = has_left.astype(jnp.int32) + has_right.astype(jnp.int32)

    def rows_of(place):
        return pl.ds(pl.multiple_of(place * R, R), R)

    barrier = pltpu.get_barrier_semaphore()
    for r in range(D - 1, 0, -1):
        pl.semaphore_signal(barrier, inc=1, device_id={"date": flipped(date, r)}, device_id_type=MESH)

    @pl.when(jnp.logical_not(odd) & has_right)
    def _():
        for r in range(D - 1, -1, -1):
            pl.semaphore_signal(barrier, inc=1, device_id={"date": flipped(date, r), "col": col + 1}, device_id_type=MESH)

    @pl.when(jnp.logical_not(odd) & has_left)
    def _():
        for r in range(D - 1, -1, -1):
            pl.semaphore_signal(barrier, inc=1, device_id={"date": flipped(date, r), "col": col - 1}, device_id_type=MESH)

    load = pltpu.make_async_copy(scenes, local, load_sem)
    load.start()
    own = [
        pltpu.make_async_copy(dates, dates_in.at[date], own_sem.at[0]),
        pltpu.make_async_copy(count, counts_in.at[date], own_sem.at[1]),
        pltpu.make_async_copy(inverse, inverse_in, own_sem.at[2]),
    ]
    for copy in own:
        copy.start()

    def remote(src, dst, ssem, rsem, device):
        return pltpu.make_async_remote_copy(src_ref=src, dst_ref=dst, send_sem=ssem, recv_sem=rsem, device_id=device, device_id_type=MESH)

    def chunk(n):
        return n // H * W, n % H

    def send_far(n):
        t, h = chunk(n)
        for r in (2, 3):
            there = flipped(date, r)
            rows = pl.ds(pl.multiple_of(there * R + h * SUBLANES, SUBLANES), SUBLANES)
            remote(scenes.at[:, :, rows, t * LANES:(t + W) * LANES], far.at[n, r - 2], far_send, far_recv.at[n], {"date": there}).start()

    partner = flipped(date, 1)
    to_near = remote(scenes.at[:, :, rows_of(partner), :], near, near_send, near_recv, {"date": partner})

    def send_scenes():
        send_far(0)
        to_near.start()
        for r in range(D - 1, 0, -1):
            remote(dates, dates_in.at[date], dates_send, dates_recv, {"date": flipped(date, r)}).start()
            remote(count, counts_in.at[date], count_send, count_recv, {"date": flipped(date, r)}).start()
        for n in range(1, K):
            send_far(n)

    @pl.when(jnp.logical_not(odd))
    def _():
        pl.semaphore_wait(barrier, D - 1)
        send_scenes()

    @pl.when(jnp.logical_not(has_left))
    def _():
        edge_in[0] = jnp.zeros(edge_in.shape[1:], BF16)

    @pl.when(jnp.logical_not(has_right))
    def _():
        edge_in[1] = jnp.zeros(edge_in.shape[1:], BF16)

    load.wait()
    lane = iota((D * R, LANES), 1)
    packed = jnp.zeros((D * R, LANES), F32)
    for i in range(2 * A):
        first = local[i // 2, i % 2, :, 0:LANES].astype(F32)
        last = local[i // 2, i % 2, :, X - LANES:X].astype(F32)
        shift = 2 * EDGE * i + EDGE
        packed = jnp.where(lane // EDGE == 2 * i, pltpu.roll(last, shift, 1), packed)
        packed = jnp.where(lane // EDGE == 2 * i + 1, pltpu.roll(first, shift, 1), packed)
    packed = jnp.concatenate([packed, jnp.zeros((LANES - D * R, LANES), F32)], axis=0)
    turned[...] = jnp.transpose(packed)
    spot = iota((2 * A, LANES), 1) // R
    columns = [turned[pl.ds(n, 2 * A, stride=2 * EDGE), :] for n in range(2 * EDGE)]
    for side in range(2):
        for d in range(D):
            total = jnp.zeros((2 * A, LANES), F32)
            for n in range(side * EDGE, (side + 1) * EDGE):
                shift = (n * R - d * R) % LANES
                total = jnp.where(spot == n, pltpu.roll(columns[n], shift, 1) if shift else columns[n], total)
            edge_out[side, d] = total.astype(BF16)

    def to_side(side, r):
        there = flipped(date, r)
        return remote(edge_out.at[side, there], edge_in.at[side, r], edge_send.at[side], edge_recv.at[side], {"date": there, "col": col + 1 - 2 * side})

    def send_edges(chosen):
        @pl.when(chosen & has_right)
        def _():
            for r in range(D - 1, -1, -1):
                to_side(0, r).start()

        @pl.when(chosen & has_left)
        def _():
            for r in range(D - 1, -1, -1):
                to_side(1, r).start()

    @pl.when(odd)
    def _():
        pl.semaphore_wait(barrier, D - 1 + D * sides)

    @pl.when(odd & has_left)
    def _():
        pl.semaphore_signal(met_sem, inc=1, device_id={"col": col - 1}, device_id_type=MESH)

    @pl.when(odd & has_right)
    def _():
        pl.semaphore_signal(met_sem, inc=1, device_id={"col": col + 1}, device_id_type=MESH)

    send_edges(odd)

    @pl.when(odd)
    def _():
        send_scenes()

    row = iota(((T + 1) * LANES, LANES), 0)
    at = row - T * LANES
    place = at // R
    column = jnp.where(at < 0, row, jnp.where(place < EDGE, place - EDGE, place - EDGE + X))
    target = iota(((T + 1) * LANES, LANES), 1)
    offset = column - 8 * target + 4
    inside = (target < looks) & (offset >= 0) & (offset < 16)
    weights[...] = jnp.where(inside, (8.0 - jnp.abs(offset.astype(F32) - 7.5)) / 128.0, 0.0).astype(BF16)

    def unpack(raw, pitch, again, c, t, h, index, block):
        start = ((c * T + t) * R + h * SUBLANES) * pitch + index
        raw[pl.ds(start, SUBLANES, stride=pitch), :] = block
        if index < again:
            raw[pl.ds(start + group, SUBLANES, stride=pitch), :] = block

    def unpack_near(of, slot):
        for c in range(2):
            for t in range(T):
                for i in range(A):
                    both = of(i, c, t).astype(F32)
                    for h in range(H):
                        unpack(raw_a, pitch_a, group // 2, c, t, h, slot * A + i, both[h * SUBLANES:(h + 1) * SUBLANES])

    def got(raw, pitch, c, t, r, parity, turn):
        start = ((c * T + t) * R + 2 * r + parity) * pitch + turn
        return raw[pl.ds(start, group), :]

    def four(raw, pitch, t, r, turn):
        return [got(raw, pitch, c, t, r, parity, turn) for parity in range(2) for c in range(2)]

    def product(p, s):
        real = imaginary = None
        for n in range(0, len(p), 2):
            one = p[n] * s[n] + p[n + 1] * s[n + 1]
            two = p[n + 1] * s[n] - p[n] * s[n + 1]
            real = one if real is None else real + one
            imaginary = two if imaginary is None else imaginary + two
        return real, imaginary

    def emit(into, c, at, lanes, values):
        high, low = split(jnp.concatenate(values, axis=0))
        into[c, at:at + 2 * group, lanes] = high
        into[c, height + at:height + at + 2 * group, lanes] = low

    def run(into, lanes, load_of, steps):
        firsts = {}
        for n in steps:
            both = []
            for g, k, turn in order[2 * n:2 * n + 2]:
                if g not in firsts:
                    firsts[g] = load_of(g, 0)
                both.append(product(firsts[g], load_of(k, turn)))
            for c in range(2):
                emit(into, c, 2 * n * group, lanes, [v[c] for v in both])

    def part_of(n, steps):
        t, h = chunk(n)
        for u in range(W):
            for i in range(part):
                r = h * part + i

                def load_of(g, turn):
                    return four(raw_b, pitch_b, t + u, r, turn) if g else four(raw_a, pitch_a, t + u, r, turn)

                at = (u * part + i) * LANES
                run(pairs.at[n], slice(at, at + LANES), load_of, steps)

    def contract(c, rhs):
        value = jnp.dot(coef[c], rhs, preferred_element_type=F32)
        return value[0:QP] + value[QP:2 * QP]

    early = group // 4
    steps = len(order) // 2

    unpack_near(lambda i, c, t: local[i, c, rows_of(date), t * LANES:(t + 1) * LANES], 0)
    @pl.when(jnp.logical_not(odd))
    def _():
        pl.semaphore_wait(met_sem, sides)

    send_edges(jnp.logical_not(odd))

    to_near.wait_recv()
    unpack_near(lambda i, c, t: near[i, c, :, t * LANES:(t + 1) * LANES], 1)
    for n in range(K):
        part_of(n, range(early))

    for copy in own:
        copy.wait()
    others = pl.ds(0, D - 1)
    pltpu.make_async_copy(dates_in.at[others], dates_in.at[others], dates_recv).wait()
    pltpu.make_async_copy(counts_in.at[others], counts_in.at[others], count_recv).wait()
    coefficients(cfg, date, order, dates_in, counts_in, inverse_in, coef)

    for n in range(K):
        t, h = chunk(n)
        pltpu.make_async_copy(far.at[n], far.at[n], far_recv.at[n]).wait()
        for slot in range(2):
            for i in range(A):
                for c in range(2):
                    for u in range(W):
                        block = far[n, slot, i, c, :, u * LANES:(u + 1) * LANES].astype(F32)
                        unpack(raw_b, pitch_b, group - 1, c, t + u, h, slot * A + i, block)
        part_of(n, range(early, steps))
        for c in range(2):
            value = contract(c, pairs[n, c])
            for u in range(W):
                for i in range(part):
                    start = (h * part + i) * pitch_r + c * QP
                    at = (u * part + i) * LANES
                    along[t + u, start:start + QP] = value[:, at:at + LANES]

    @pl.when(has_left)
    def _():
        pltpu.make_async_copy(edge_in.at[0], edge_in.at[0], edge_recv.at[0]).wait()

    @pl.when(has_right)
    def _():
        pltpu.make_async_copy(edge_in.at[1], edge_in.at[1], edge_recv.at[1]).wait()

    for slot in range(D):
        value = edge_in[0, slot].astype(F32) + edge_in[1, slot].astype(F32)
        start = slot // 2 * 4 * group + slot % 2 * 2 * A
        raw_e[start:start + 2 * A] = value
        raw_e[start + 2 * group:start + 2 * group + 2 * A] = value

    def edges_of(g, turn):
        return [raw_e[pl.ds(g * 4 * group + c + 2 * turn, group, stride=2), :] for c in range(2)]

    run(pairs_e, slice(0, LANES), edges_of, range(steps))
    for c in range(2):
        along_e[c * QP:(c + 1) * QP] = contract(c, pairs_e[c])

    mine = (iota((half, LANES), 1) % R) // 2 == iota((half, LANES), 0)
    blocks = []
    for q in range(NP):
        for c in range(2):
            main = [along[t, pl.ds(c * QP + q, half, stride=pitch_r), :] for t in range(T)]
            edge = jnp.where(mine, along_e[pl.ds(c * QP + q, half, stride=0), :], 0.0)
            blocks.append(jnp.concatenate(main + [edge], axis=1))
    high, low = split(jnp.concatenate(blocks, axis=0))
    series = jnp.dot(high, weights[...], preferred_element_type=F32)
    series = series + jnp.dot(low, weights[...], preferred_element_type=F32)
    out[...] = series[:, 0:looks].reshape(NP, 2, half, looks)

    pltpu.make_async_copy(far, far, far_send).wait()
    to_near.wait_send()
    pltpu.make_async_copy(dates_in.at[others], dates_in.at[others], dates_send).wait()
    pltpu.make_async_copy(counts_in.at[others], counts_in.at[others], count_send).wait()

    @pl.when(has_right)
    def _():
        pltpu.make_async_copy(edge_out.at[0], edge_out.at[0], edge_send.at[0]).wait()

    @pl.when(has_left)
    def _():
        pltpu.make_async_copy(edge_out.at[1], edge_out.at[1], edge_send.at[1]).wait()


def coefficients(cfg, date, order, dates_in, counts_in, inverse, coef):
    D, A, S, NP = (cfg[k] for k in ("D", "A", "S", "NP"))
    total = D * A
    group = D // 2 * A
    height = len(order) * group
    codes = []
    for d in range(D):
        row = dates_in[d, 0:1, :] * total + dates_in[d, 1:2, :]
        live = iota((1, S), 1) < counts_in[d]
        codes.append(jnp.where(live, row, -1).astype(F32))
    codes.append(jnp.full((SUBLANES - D, S), -1.0, F32))
    table = jnp.concatenate(codes, axis=0)
    table = jnp.concatenate([table, jnp.full((SUBLANES, LANES - S), -1.0, F32)], axis=1)
    spun = jnp.transpose(table)
    code = jnp.concatenate([spun[0:S, d:d + 1] for d in range(D)], axis=0).astype(jnp.int32)

    place = iota((1, height), 1)
    index = place % group
    first, second, valid = index, index, index >= 0
    for n, (g, k, turn) in enumerate(order):
        here = place // group == n
        first = jnp.where(here, g * group + index, first)
        second = jnp.where(here, k * group + (index + turn) % group, second)
        if g == k and 2 * turn == group:
            valid = valid & jnp.logical_not(here & (index >= turn))
    first = flipped(date, first // A) * A + first % A
    second = flipped(date, second // A) * A + second % A
    ahead = first < second
    want = jnp.where(ahead, first * total + second, second * total + first)
    want = jnp.where(valid, want, -2)
    hit = jnp.where(code == want, 1.0, 0.0).astype(BF16)
    high, low = split(jnp.concatenate([inverse[...], jnp.zeros((2 * SUBLANES - NP, D * S), F32)], axis=0))
    value = jnp.dot(high, hit, preferred_element_type=F32) + jnp.dot(low, hit, preferred_element_type=F32)
    for c in range(2):
        high, low = split(value if c == 0 else jnp.where(ahead, value, -value))
        top = jnp.concatenate([high, high], axis=1)
        bottom = jnp.concatenate([low, jnp.zeros_like(low)], axis=1)
        coef[c] = jnp.concatenate([top, bottom], axis=0)


def padded(cells, sides, width):
    for axis, dim in sides:
        count = lax.axis_size(axis)
        ends = count - 1
        head = lax.slice_in_dim(cells, 0, width, axis=dim)
        tail = lax.slice_in_dim(cells, cells.shape[dim] - width, cells.shape[dim], axis=dim)
        cells = jnp.concatenate(
            [
                lax.ppermute(tail, axis, [(i, (i + 1) % count) for i in range(ends)]),
                cells,
                lax.ppermute(head, axis, [((i + 1) % count, i) for i in range(ends)]),
            ],
            axis=dim,
        )
    return cells


def look_matrix(padded_width, looks_here):
    column = jnp.arange(padded_width, dtype=jnp.int32)[:, None]
    target = jnp.arange(looks_here, dtype=jnp.int32)[None, :]
    offset = (column - 8 * target).astype(jnp.float32)
    inside = (offset >= 0.0) & (offset < 16.0)
    return jnp.where(inside, (8.0 - jnp.abs(offset - 7.5)) / 64.0, 0.0)


def plain_device(scenes, pair_dates, pair_count, inverse):
    slot_count = pair_dates.shape[0]
    looks_here = scenes.shape[3] // 8
    base = lax.all_to_all(scenes, "date", split_axis=2, concat_axis=0, tiled=True)
    used_dates, used_counts = (
        lax.all_gather(pair_dates, "date", axis=0, tiled=True),
        lax.all_gather(pair_count, "date", axis=0, tiled=True),
    )
    slot_index = jnp.arange(used_dates.shape[0], dtype=jnp.int32)
    living = (slot_index % slot_count < jnp.take(used_counts, slot_index // slot_count)).astype(
        jnp.float32
    )
    primary = jnp.take(base, used_dates[:, 0], axis=0)
    secondary = jnp.take(base, used_dates[:, 1], axis=0)
    p_real = primary[:, 0].astype(jnp.float32)
    p_imag = primary[:, 1].astype(jnp.float32)
    s_real = secondary[:, 0].astype(jnp.float32)
    s_imag = secondary[:, 1].astype(jnp.float32)
    real_part = p_real * s_real + p_imag * s_imag
    imaginary = p_imag * s_real - p_real * s_imag
    products = jnp.stack([real_part, imaginary], axis=1) * living[:, None, None, None]
    products = padded(products, (("col", 3),), 4)
    pair_total = products.shape[0]
    padded_width = products.shape[3]
    half_rows = products.shape[2] // 2
    halved = products.reshape(pair_total, 2, half_rows, 2, padded_width).sum(axis=3) * 0.5
    looked = jnp.dot(
        halved.reshape(-1, padded_width),
        look_matrix(padded_width, looks_here),
        precision=lax.Precision.HIGHEST,
        preferred_element_type=jnp.float32,
    )
    looked = looked.reshape(pair_total, 2, half_rows, looks_here)
    return jnp.einsum("qk,kcrm->qcrm", inverse, looked, precision=lax.Precision.HIGHEST)


def per_device(scenes, pair_dates, pair_count, inverse):
    D, C = lax.axis_size("date"), lax.axis_size("col")
    A, _, rows, X = scenes.shape
    S, NP = pair_dates.shape[0], inverse.shape[0]
    R = rows // D
    half = R // 2
    fits = D == 4 and 2 * A == SUBLANES and R == 2 * SUBLANES and X % LANES == 0 and X // 8 <= LANES and X <= 4 * LANES
    fits = fits and S % 8 == 0 and S <= LANES and NP <= 2 * SUBLANES and rows <= LANES
    if not fits:
        return plain_device(scenes, pair_dates, pair_count, inverse)
    T, H = X // LANES, R // SUBLANES
    W = 1
    K = T // W * H
    group = D // 2 * A
    height = len(turns(group)) * group
    cfg = dict(D=D, C=C, A=A, R=R, X=X, S=S, NP=NP, pitch_a=group + group // 2 + 1, pitch_b=2 * group - 1, pitch_r=4 * SUBLANES + 1, W=W)
    dma, regular = pltpu.SemaphoreType.DMA, pltpu.SemaphoreType.REGULAR
    return pl.pallas_call(
        functools.partial(stack_kernel, cfg),
        out_shape=pltpu.VMEM((NP, 2, half, X // 8), F32),
        in_specs=[pl.BlockSpec(memory_space=pltpu.HBM)] * 4,
        out_specs=pl.BlockSpec(memory_space=pltpu.VMEM),
        scratch_shapes=[
            pltpu.VMEM(scenes.shape, BF16),
            pltpu.VMEM((A, 2, R, X), BF16),
            pltpu.VMEM((K, 2, A, 2, SUBLANES, W * LANES), BF16),
            pltpu.VMEM((D, 2, S), jnp.int32),
            pltpu.VMEM((D, 1, 1), jnp.int32),
            pltpu.VMEM(inverse.shape, F32),
            pltpu.VMEM((2, D, 2 * A, LANES), BF16),
            pltpu.VMEM((2, D, 2 * A, LANES), BF16),
            pltpu.VMEM((LANES, LANES), F32),
            pltpu.VMEM((2 * T * R * cfg["pitch_a"], LANES), F32),
            pltpu.VMEM((2 * T * R * cfg["pitch_b"], LANES), F32),
            pltpu.VMEM((8 * group, LANES), F32),
            pltpu.VMEM((K, 2, 2 * height, SUBLANES // 2 * W * LANES), BF16),
            pltpu.VMEM((2, 2 * height, LANES), BF16),
            pltpu.VMEM(((T + 1) * LANES, LANES), BF16),
            pltpu.VMEM((2, 4 * SUBLANES, 2 * height), BF16),
            pltpu.VMEM((T, half * cfg["pitch_r"], LANES), F32),
            pltpu.VMEM((4 * SUBLANES, LANES), F32),
            dma, dma((3,)), dma, dma((K,)), dma, dma,
            dma, dma, dma, dma, dma((2,)), dma((2,)), regular,
        ],
        compiler_params=pltpu.CompilerParams(collective_id=0, has_side_effects=True),
    )(scenes, pair_dates.T, pair_count.reshape(1, 1), inverse)


def solution(mesh):
    placed = (P("date", None, "groups", "col"), P("date", None), P("date"), P())
    return jax.shard_map(
        per_device,
        mesh=mesh,
        in_specs=placed,
        out_specs=P(None, None, ("groups", "date"), "col"),
        check_vma=False,
    )
```

```python
import functools

import jax
import jax.numpy as jnp
from jax import lax
from jax.experimental import pallas as pl
from jax.experimental.pallas import tpu as pltpu
from jax.sharding import PartitionSpec as P

MESH = pl.DeviceIdType.MESH
F32 = jnp.float32
BF16 = jnp.bfloat16
EDGE = 4
LANES = 128
SUBLANES = 8


def flipped(place, slot):
    low, high = place % 2, place // 2
    a, b = slot % 2, slot // 2
    return low + a - 2 * low * a + 2 * (high + b - 2 * high * b)


def split(value):
    high = value.astype(BF16)
    return high, (value - high.astype(F32)).astype(BF16)


def iota(shape, dim):
    return lax.broadcasted_iota(jnp.int32, shape, dim)


def turns(group):
    half = group // 2
    inside = [(g, g, n) for g in range(2) for n in range(1, half + 1)]
    return inside[:half] + [(0, 1, n) for n in range(group)] + inside[half:]


def stack_kernel(
    cfg,
    scenes, dates, count, inverse, out,
    local, near, far, dates_in, counts_in, inverse_in, edge_out, edge_in, turned,
    raw_a, raw_b, raw_e, pairs, pairs_e, weights, coef, along, along_e,
    load_sem, own_sem, far_send, far_recv, near_send, near_recv,
    dates_send, dates_recv, count_send, count_recv, edge_send, edge_recv, met_sem,
):
    D, C, A, R, X, S, NP = (cfg[k] for k in ("D", "C", "A", "R", "X", "S", "NP"))
    T = X // LANES
    H = R // SUBLANES
    half = R // 2
    part = SUBLANES // 2
    W = cfg["W"]
    K = T // W * H
    looks = X // 8
    group = D // 2 * A
    order = turns(group)
    height = len(order) * group
    QP = 2 * SUBLANES
    pitch_a, pitch_b, pitch_r = cfg["pitch_a"], cfg["pitch_b"], cfg["pitch_r"]
    date = lax.axis_index("date")
    col = lax.axis_index("col")
    has_left = col > 0
    has_right = col < C - 1
    odd = col % 2 == 1
    sides = has_left.astype(jnp.int32) + has_right.astype(jnp.int32)

    def rows_of(place):
        return pl.ds(pl.multiple_of(place * R, R), R)

    barrier = pltpu.get_barrier_semaphore()
    for r in range(D - 1, 0, -1):
        pl.semaphore_signal(barrier, inc=1, device_id={"date": flipped(date, r)}, device_id_type=MESH)

    @pl.when(jnp.logical_not(odd) & has_right)
    def _():
        for r in range(D - 1, -1, -1):
            pl.semaphore_signal(barrier, inc=1, device_id={"date": flipped(date, r), "col": col + 1}, device_id_type=MESH)

    @pl.when(jnp.logical_not(odd) & has_left)
    def _():
        for r in range(D - 1, -1, -1):
            pl.semaphore_signal(barrier, inc=1, device_id={"date": flipped(date, r), "col": col - 1}, device_id_type=MESH)

    load = pltpu.make_async_copy(scenes, local, load_sem)
    load.start()
    own = [
        pltpu.make_async_copy(dates, dates_in.at[date], own_sem.at[0]),
        pltpu.make_async_copy(count, counts_in.at[date], own_sem.at[1]),
        pltpu.make_async_copy(inverse, inverse_in, own_sem.at[2]),
    ]
    for copy in own:
        copy.start()

    def remote(src, dst, ssem, rsem, device):
        return pltpu.make_async_remote_copy(src_ref=src, dst_ref=dst, send_sem=ssem, recv_sem=rsem, device_id=device, device_id_type=MESH)

    def chunk(n):
        return n // H * W, n % H

    def send_far(n):
        t, h = chunk(n)
        for r in (2, 3):
            there = flipped(date, r)
            rows = pl.ds(pl.multiple_of(there * R + h * SUBLANES, SUBLANES), SUBLANES)
            for i in range(A):
                some = slice(i, i + 1)
                remote(scenes.at[some, :, rows, t * LANES:(t + W) * LANES], far.at[n, r - 2, some], far_send, far_recv.at[n], {"date": there}).start()

    partner = flipped(date, 1)
    to_near = remote(scenes.at[:, :, rows_of(partner), :], near, near_send, near_recv, {"date": partner})

    def send_scenes():
        send_far(0)
        to_near.start()
        for r in range(D - 1, 0, -1):
            remote(dates, dates_in.at[date], dates_send, dates_recv, {"date": flipped(date, r)}).start()
            remote(count, counts_in.at[date], count_send, count_recv, {"date": flipped(date, r)}).start()
        for n in range(1, K):
            send_far(n)

    @pl.when(jnp.logical_not(odd))
    def _():
        pl.semaphore_wait(barrier, D - 1)
        send_scenes()

    @pl.when(jnp.logical_not(has_left))
    def _():
        edge_in[0] = jnp.zeros(edge_in.shape[1:], BF16)

    @pl.when(jnp.logical_not(has_right))
    def _():
        edge_in[1] = jnp.zeros(edge_in.shape[1:], BF16)

    load.wait()
    lane = iota((D * R, LANES), 1)
    packed = jnp.zeros((D * R, LANES), F32)
    for i in range(2 * A):
        first = local[i // 2, i % 2, :, 0:LANES].astype(F32)
        last = local[i // 2, i % 2, :, X - LANES:X].astype(F32)
        shift = 2 * EDGE * i + EDGE
        packed = jnp.where(lane // EDGE == 2 * i, pltpu.roll(last, shift, 1), packed)
        packed = jnp.where(lane // EDGE == 2 * i + 1, pltpu.roll(first, shift, 1), packed)
    packed = jnp.concatenate([packed, jnp.zeros((LANES - D * R, LANES), F32)], axis=0)
    turned[...] = jnp.transpose(packed)
    spot = iota((2 * A, LANES), 1) // R
    columns = [turned[pl.ds(n, 2 * A, stride=2 * EDGE), :] for n in range(2 * EDGE)]
    for side in range(2):
        for d in range(D):
            total = jnp.zeros((2 * A, LANES), F32)
            for n in range(side * EDGE, (side + 1) * EDGE):
                shift = (n * R - d * R) % LANES
                total = jnp.where(spot == n, pltpu.roll(columns[n], shift, 1) if shift else columns[n], total)
            edge_out[side, d] = total.astype(BF16)

    def to_side(side, r):
        there = flipped(date, r)
        return remote(edge_out.at[side, there], edge_in.at[side, r], edge_send.at[side], edge_recv.at[side], {"date": there, "col": col + 1 - 2 * side})

    def send_edges(chosen):
        @pl.when(chosen & has_right)
        def _():
            for r in range(D - 1, -1, -1):
                to_side(0, r).start()

        @pl.when(chosen & has_left)
        def _():
            for r in range(D - 1, -1, -1):
                to_side(1, r).start()

    @pl.when(odd)
    def _():
        pl.semaphore_wait(barrier, D - 1 + D * sides)

    @pl.when(odd & has_left)
    def _():
        pl.semaphore_signal(met_sem, inc=1, device_id={"col": col - 1}, device_id_type=MESH)

    @pl.when(odd & has_right)
    def _():
        pl.semaphore_signal(met_sem, inc=1, device_id={"col": col + 1}, device_id_type=MESH)

    send_edges(odd)

    @pl.when(odd)
    def _():
        send_scenes()

    row = iota(((T + 1) * LANES, LANES), 0)
    at = row - T * LANES
    place = at // R
    column = jnp.where(at < 0, row, jnp.where(place < EDGE, place - EDGE, place - EDGE + X))
    target = iota(((T + 1) * LANES, LANES), 1)
    offset = column - 8 * target + 4
    inside = (target < looks) & (offset >= 0) & (offset < 16)
    weights[...] = jnp.where(inside, (8.0 - jnp.abs(offset.astype(F32) - 7.5)) / 128.0, 0.0).astype(BF16)

    def unpack(raw, pitch, again, c, t, h, index, block):
        start = ((c * T + t) * R + h * SUBLANES) * pitch + index
        raw[pl.ds(start, SUBLANES, stride=pitch), :] = block
        if index < again:
            raw[pl.ds(start + group, SUBLANES, stride=pitch), :] = block

    def unpack_near(of, slot):
        for c in range(2):
            for t in range(T):
                for i in range(A):
                    both = of(i, c, t).astype(F32)
                    for h in range(H):
                        unpack(raw_a, pitch_a, group // 2, c, t, h, slot * A + i, both[h * SUBLANES:(h + 1) * SUBLANES])

    def got(raw, pitch, c, t, r, parity, turn):
        start = ((c * T + t) * R + 2 * r + parity) * pitch + turn
        return raw[pl.ds(start, group), :]

    def four(raw, pitch, t, r, turn):
        return [got(raw, pitch, c, t, r, parity, turn) for parity in range(2) for c in range(2)]

    def product(p, s):
        real = imaginary = None
        for n in range(0, len(p), 2):
            one = p[n] * s[n] + p[n + 1] * s[n + 1]
            two = p[n + 1] * s[n] - p[n] * s[n + 1]
            real = one if real is None else real + one
            imaginary = two if imaginary is None else imaginary + two
        return real, imaginary

    def emit(into, c, at, lanes, values):
        high, low = split(jnp.concatenate(values, axis=0))
        into[c, at:at + 2 * group, lanes] = high
        into[c, height + at:height + at + 2 * group, lanes] = low

    def run(into, lanes, load_of, steps):
        firsts = {}
        for n in steps:
            both = []
            for g, k, turn in order[2 * n:2 * n + 2]:
                if g not in firsts:
                    firsts[g] = load_of(g, 0)
                both.append(product(firsts[g], load_of(k, turn)))
            for c in range(2):
                emit(into, c, 2 * n * group, lanes, [v[c] for v in both])

    def part_of(n, steps):
        t, h = chunk(n)
        for u in range(W):
            for i in range(part):
                r = h * part + i

                def load_of(g, turn):
                    return four(raw_b, pitch_b, t + u, r, turn) if g else four(raw_a, pitch_a, t + u, r, turn)

                at = (u * part + i) * LANES
                run(pairs.at[n], slice(at, at + LANES), load_of, steps)

    def contract(c, rhs):
        value = jnp.dot(coef[c], rhs, preferred_element_type=F32)
        return value[0:QP] + value[QP:2 * QP]

    early = group // 4
    steps = len(order) // 2

    unpack_near(lambda i, c, t: local[i, c, rows_of(date), t * LANES:(t + 1) * LANES], 0)
    @pl.when(jnp.logical_not(odd))
    def _():
        pl.semaphore_wait(met_sem, sides)

    send_edges(jnp.logical_not(odd))

    to_near.wait_recv()
    unpack_near(lambda i, c, t: near[i, c, :, t * LANES:(t + 1) * LANES], 1)
    for n in range(K):
        part_of(n, range(early))

    for copy in own:
        copy.wait()
    others = pl.ds(0, D - 1)
    pltpu.make_async_copy(dates_in.at[others], dates_in.at[others], dates_recv).wait()
    pltpu.make_async_copy(counts_in.at[others], counts_in.at[others], count_recv).wait()
    coefficients(cfg, date, order, dates_in, counts_in, inverse_in, coef)

    for n in range(K):
        t, h = chunk(n)
        pltpu.make_async_copy(far.at[n], far.at[n], far_recv.at[n]).wait()
        for slot in range(2):
            for i in range(A):
                for c in range(2):
                    for u in range(W):
                        block = far[n, slot, i, c, :, u * LANES:(u + 1) * LANES].astype(F32)
                        unpack(raw_b, pitch_b, group - 1, c, t + u, h, slot * A + i, block)
        part_of(n, range(early, steps))
        for c in range(2):
            value = contract(c, pairs[n, c])
            for u in range(W):
                for i in range(part):
                    start = (h * part + i) * pitch_r + c * QP
                    at = (u * part + i) * LANES
                    along[t + u, start:start + QP] = value[:, at:at + LANES]

    @pl.when(has_left)
    def _():
        pltpu.make_async_copy(edge_in.at[0], edge_in.at[0], edge_recv.at[0]).wait()

    @pl.when(has_right)
    def _():
        pltpu.make_async_copy(edge_in.at[1], edge_in.at[1], edge_recv.at[1]).wait()

    for slot in range(D):
        value = edge_in[0, slot].astype(F32) + edge_in[1, slot].astype(F32)
        start = slot // 2 * 4 * group + slot % 2 * 2 * A
        raw_e[start:start + 2 * A] = value
        raw_e[start + 2 * group:start + 2 * group + 2 * A] = value

    def edges_of(g, turn):
        return [raw_e[pl.ds(g * 4 * group + c + 2 * turn, group, stride=2), :] for c in range(2)]

    run(pairs_e, slice(0, LANES), edges_of, range(steps))
    for c in range(2):
        along_e[c * QP:(c + 1) * QP] = contract(c, pairs_e[c])

    mine = (iota((half, LANES), 1) % R) // 2 == iota((half, LANES), 0)
    blocks = []
    for q in range(NP):
        for c in range(2):
            main = [along[t, pl.ds(c * QP + q, half, stride=pitch_r), :] for t in range(T)]
            edge = jnp.where(mine, along_e[pl.ds(c * QP + q, half, stride=0), :], 0.0)
            blocks.append(jnp.concatenate(main + [edge], axis=1))
    high, low = split(jnp.concatenate(blocks, axis=0))
    both = jnp.dot(jnp.concatenate([high, low], axis=0), weights[...], preferred_element_type=F32)
    series = both[0:2 * NP * half] + both[2 * NP * half:]
    out[...] = series[:, 0:looks].reshape(NP, 2, half, looks)

    pltpu.make_async_copy(far, far, far_send).wait()
    to_near.wait_send()
    pltpu.make_async_copy(dates_in.at[others], dates_in.at[others], dates_send).wait()
    pltpu.make_async_copy(counts_in.at[others], counts_in.at[others], count_send).wait()

    @pl.when(has_right)
    def _():
        pltpu.make_async_copy(edge_out.at[0], edge_out.at[0], edge_send.at[0]).wait()

    @pl.when(has_left)
    def _():
        pltpu.make_async_copy(edge_out.at[1], edge_out.at[1], edge_send.at[1]).wait()


def coefficients(cfg, date, order, dates_in, counts_in, inverse, coef):
    D, A, S, NP = (cfg[k] for k in ("D", "A", "S", "NP"))
    total = D * A
    group = D // 2 * A
    height = len(order) * group
    codes = []
    for d in range(D):
        row = dates_in[d, 0:1, :] * total + dates_in[d, 1:2, :]
        live = iota((1, S), 1) < counts_in[d]
        codes.append(jnp.where(live, row, -1).astype(F32))
    codes.append(jnp.full((SUBLANES - D, S), -1.0, F32))
    table = jnp.concatenate(codes, axis=0)
    table = jnp.concatenate([table, jnp.full((SUBLANES, LANES - S), -1.0, F32)], axis=1)
    spun = jnp.transpose(table)
    code = jnp.concatenate([spun[0:S, d:d + 1] for d in range(D)], axis=0).astype(jnp.int32)

    place = iota((1, height), 1)
    index = place % group
    first, second, valid = index, index, index >= 0
    for n, (g, k, turn) in enumerate(order):
        here = place // group == n
        first = jnp.where(here, g * group + index, first)
        second = jnp.where(here, k * group + (index + turn) % group, second)
        if g == k and 2 * turn == group:
            valid = valid & jnp.logical_not(here & (index >= turn))
    first = flipped(date, first // A) * A + first % A
    second = flipped(date, second // A) * A + second % A
    ahead = first < second
    want = jnp.where(ahead, first * total + second, second * total + first)
    want = jnp.where(valid, want, -2)
    hit = jnp.where(code == want, 1.0, 0.0).astype(BF16)
    high, low = split(jnp.concatenate([inverse[...], jnp.zeros((2 * SUBLANES - NP, D * S), F32)], axis=0))
    value = jnp.dot(high, hit, preferred_element_type=F32) + jnp.dot(low, hit, preferred_element_type=F32)
    for c in range(2):
        high, low = split(value if c == 0 else jnp.where(ahead, value, -value))
        top = jnp.concatenate([high, high], axis=1)
        bottom = jnp.concatenate([low, jnp.zeros_like(low)], axis=1)
        coef[c] = jnp.concatenate([top, bottom], axis=0)


def padded(cells, sides, width):
    for axis, dim in sides:
        count = lax.axis_size(axis)
        ends = count - 1
        head = lax.slice_in_dim(cells, 0, width, axis=dim)
        tail = lax.slice_in_dim(cells, cells.shape[dim] - width, cells.shape[dim], axis=dim)
        cells = jnp.concatenate(
            [
                lax.ppermute(tail, axis, [(i, (i + 1) % count) for i in range(ends)]),
                cells,
                lax.ppermute(head, axis, [((i + 1) % count, i) for i in range(ends)]),
            ],
            axis=dim,
        )
    return cells


def look_matrix(padded_width, looks_here):
    column = jnp.arange(padded_width, dtype=jnp.int32)[:, None]
    target = jnp.arange(looks_here, dtype=jnp.int32)[None, :]
    offset = (column - 8 * target).astype(jnp.float32)
    inside = (offset >= 0.0) & (offset < 16.0)
    return jnp.where(inside, (8.0 - jnp.abs(offset - 7.5)) / 64.0, 0.0)


def plain_device(scenes, pair_dates, pair_count, inverse):
    slot_count = pair_dates.shape[0]
    looks_here = scenes.shape[3] // 8
    base = lax.all_to_all(scenes, "date", split_axis=2, concat_axis=0, tiled=True)
    used_dates, used_counts = (
        lax.all_gather(pair_dates, "date", axis=0, tiled=True),
        lax.all_gather(pair_count, "date", axis=0, tiled=True),
    )
    slot_index = jnp.arange(used_dates.shape[0], dtype=jnp.int32)
    living = (slot_index % slot_count < jnp.take(used_counts, slot_index // slot_count)).astype(
        jnp.float32
    )
    primary = jnp.take(base, used_dates[:, 0], axis=0)
    secondary = jnp.take(base, used_dates[:, 1], axis=0)
    p_real = primary[:, 0].astype(jnp.float32)
    p_imag = primary[:, 1].astype(jnp.float32)
    s_real = secondary[:, 0].astype(jnp.float32)
    s_imag = secondary[:, 1].astype(jnp.float32)
    real_part = p_real * s_real + p_imag * s_imag
    imaginary = p_imag * s_real - p_real * s_imag
    products = jnp.stack([real_part, imaginary], axis=1) * living[:, None, None, None]
    products = padded(products, (("col", 3),), 4)
    pair_total = products.shape[0]
    padded_width = products.shape[3]
    half_rows = products.shape[2] // 2
    halved = products.reshape(pair_total, 2, half_rows, 2, padded_width).sum(axis=3) * 0.5
    looked = jnp.dot(
        halved.reshape(-1, padded_width),
        look_matrix(padded_width, looks_here),
        precision=lax.Precision.HIGHEST,
        preferred_element_type=jnp.float32,
    )
    looked = looked.reshape(pair_total, 2, half_rows, looks_here)
    return jnp.einsum("qk,kcrm->qcrm", inverse, looked, precision=lax.Precision.HIGHEST)


def per_device(scenes, pair_dates, pair_count, inverse):
    D, C = lax.axis_size("date"), lax.axis_size("col")
    A, _, rows, X = scenes.shape
    S, NP = pair_dates.shape[0], inverse.shape[0]
    R = rows // D
    half = R // 2
    fits = D == 4 and 2 * A == SUBLANES and R == 2 * SUBLANES and X % LANES == 0 and X // 8 <= LANES and X <= 4 * LANES
    fits = fits and S % 8 == 0 and S <= LANES and NP <= 2 * SUBLANES and rows <= LANES
    if not fits:
        return plain_device(scenes, pair_dates, pair_count, inverse)
    T, H = X // LANES, R // SUBLANES
    W = 1
    K = T // W * H
    group = D // 2 * A
    height = len(turns(group)) * group
    cfg = dict(D=D, C=C, A=A, R=R, X=X, S=S, NP=NP, pitch_a=group + group // 2 + 1, pitch_b=2 * group - 1, pitch_r=4 * SUBLANES + 1, W=W)
    dma, regular = pltpu.SemaphoreType.DMA, pltpu.SemaphoreType.REGULAR
    return pl.pallas_call(
        functools.partial(stack_kernel, cfg),
        out_shape=pltpu.VMEM((NP, 2, half, X // 8), F32),
        in_specs=[pl.BlockSpec(memory_space=pltpu.HBM)] * 4,
        out_specs=pl.BlockSpec(memory_space=pltpu.VMEM),
        scratch_shapes=[
            pltpu.VMEM(scenes.shape, BF16),
            pltpu.VMEM((A, 2, R, X), BF16),
            pltpu.VMEM((K, 2, A, 2, SUBLANES, W * LANES), BF16),
            pltpu.VMEM((D, 2, S), jnp.int32),
            pltpu.VMEM((D, 1, 1), jnp.int32),
            pltpu.VMEM(inverse.shape, F32),
            pltpu.VMEM((2, D, 2 * A, LANES), BF16),
            pltpu.VMEM((2, D, 2 * A, LANES), BF16),
            pltpu.VMEM((LANES, LANES), F32),
            pltpu.VMEM((2 * T * R * cfg["pitch_a"], LANES), F32),
            pltpu.VMEM((2 * T * R * cfg["pitch_b"], LANES), F32),
            pltpu.VMEM((8 * group, LANES), F32),
            pltpu.VMEM((K, 2, 2 * height, SUBLANES // 2 * W * LANES), BF16),
            pltpu.VMEM((2, 2 * height, LANES), BF16),
            pltpu.VMEM(((T + 1) * LANES, LANES), BF16),
            pltpu.VMEM((2, 4 * SUBLANES, 2 * height), BF16),
            pltpu.VMEM((T, half * cfg["pitch_r"], LANES), F32),
            pltpu.VMEM((4 * SUBLANES, LANES), F32),
            dma, dma((3,)), dma, dma((K,)), dma, dma,
            dma, dma, dma, dma, dma((2,)), dma((2,)), regular,
        ],
        compiler_params=pltpu.CompilerParams(collective_id=0, has_side_effects=True),
    )(scenes, pair_dates.T, pair_count.reshape(1, 1), inverse)


def solution(mesh):
    placed = (P("date", None, "groups", "col"), P("date", None), P("date"), P())
    return jax.shard_map(
        per_device,
        mesh=mesh,
        in_specs=placed,
        out_specs=P(None, None, ("groups", "date"), "col"),
        check_vma=False,
    )
```
